32 devices in a mesh: tok: 8 (over z, y), voc: 4 (over x, core).
Axes of the slice: x: 2, y: 2, z: 4, core: 2. Of those that a mesh axis runs over, the one named last changes fastest.
Arguments:
- teacher_rows: bfloat16 [2048, 2048], P('tok', 'voc')
- drafter_rows: bfloat16 [2048, 2048], P('tok', 'voc')
- head: bfloat16 [2048, 16384], P(None, 'voc'), may hold values from -1 to 1
- fr_ids: int32 [16384], P('voc'), may hold values from 0 to 151935, as said below
- targets: int32 [2048], P('tok'), may hold values from 0 to 151935
- dest_index: int32 [2048], P('tok'), may hold values from -1 to 2047, as said below
- counts: int32 [8], replicated, may hold values from 64 to 256, as said below
Outputs:
- row_loss: float32 [2048], P('tok')
- drafter_grad: bfloat16 [2048, 2048], P('tok', 'voc')
The draws below stay inside these ranges and needn't reach their ends.
Inputs may be any that keep to these rules, and one draw needn't show every extreme that they name: `dest_index`: the prefill rows that name a slot name distinct slots. With blocks of 256 rows and 8 blocks, a row of prefill block b names a slot of drafter block (b + k) mod 8 for k in 0, 1, 4, 5; at most 64 rows go from one prefill block to one drafter block, and every drafter block receives exactly 64 from its own prefill block. The slots named in drafter block j are exactly its first counts[j] slots, grouped by k in that order. counts[j] is the number of prefill rows that name a slot of block j; some block is full. `fr_ids`: distinct ids.
All inputs are finite; a program needn't handle non-finite values.
Results may differ from the reference program's by a relative error of at most 0.0041.
Values may be sent and summed in bfloat16 or wider, within the bound.
No kernel may reach another device: no remote copies, remote signals or barrier semaphores. Data moves between devices by JAX's collectives and lax.ppermute only.
A program may use at most 64 MiB of HBM per device.

```python
import math
import jax
import jax.numpy as jnp
from jax import lax

D = 2048
VOCAB = 151936
V = 16384
REACH = 4
ROWS_TOK = 256
ROWS = 2048
N_TOK = 8


def head_matrix(key):
    column_scale = jnp.exp(jax.random.uniform(jax.random.fold_in(key, 1), (V,), jnp.float32, math.log(0.3), math.log(3.0)))
    values = jax.random.normal(jax.random.fold_in(key, 2), (D, V), jnp.float32) * 0.05 * column_scale[None, :]
    return values.astype(jnp.bfloat16).astype(jnp.float32)


def id_list(key):
    return jax.random.permutation(jax.random.fold_in(key, 3), VOCAB)[:V].astype(jnp.int32)


def draw_head(key, part):
    return head_matrix(key).astype(jnp.bfloat16)


def draw_fr_ids(key, part):
    return id_list(key)


def draw_targets(key, part):
    listed = id_list(key)
    coin = jax.random.randint(jax.random.fold_in(key, 4), (ROWS,), 0, 10)
    chosen = jax.random.randint(jax.random.fold_in(key, 5), (ROWS,), 0, V)
    other = jax.random.randint(jax.random.fold_in(key, 6), (ROWS,), 0, VOCAB)
    return jnp.where(coin < 7, listed[chosen], other).astype(jnp.int32)


def hidden_rows(key, salt):
    inner = jax.random.fold_in(key, salt)
    row_scale = jnp.exp(jax.random.uniform(jax.random.fold_in(inner, 1), (ROWS, 1), jnp.float32, math.log(0.4), math.log(4.0)))
    base = jnp.clip(jax.random.normal(jax.random.fold_in(inner, 3), (ROWS, D), jnp.float32), -6.0, 6.0)
    rows = base * row_scale
    return rows.astype(jnp.bfloat16)


def draw_teacher_rows(key, part):
    return hidden_rows(key, 40)


def draw_drafter_rows(key, part):
    return hidden_rows(key, 41)


def packing(key):
    inner = jax.random.fold_in(key, 20)
    capacity = ROWS_TOK // REACH
    blocks = jnp.arange(N_TOK)
    reach_ids = jnp.arange(REACH)
    shifts = jnp.array([0, 1, N_TOK // 2, N_TOK // 2 + 1], jnp.int32)
    loads = jax.random.randint(jax.random.fold_in(inner, 1), (N_TOK, REACH), 1, capacity + 1)
    loads = loads.at[:, 0].set(capacity)
    full_block = jax.random.randint(jax.random.fold_in(inner, 2), (), 0, N_TOK)
    loads = jnp.where(blocks[:, None] == full_block, capacity, loads).astype(jnp.int32)
    counts = jnp.sum(loads, axis=1).astype(jnp.int32)
    offsets = jnp.cumsum(loads, axis=1) - loads
    keys = jax.random.split(jax.random.fold_in(inner, 3), N_TOK)

    def one_source(source, sub_key):
        receiver = (source + shifts) % N_TOK
        sends = loads[receiver, reach_ids]
        upper = jnp.cumsum(sends)
        lower = upper - sends
        order = jnp.arange(ROWS_TOK)
        which = jnp.sum((order[:, None] >= upper[None, :]).astype(jnp.int32), axis=1)
        capped = jnp.minimum(which, REACH - 1)
        within = order - lower[capped]
        dest_block = receiver[capped]
        place = offsets[dest_block, capped] + within
        values = jnp.where(which < REACH, dest_block * ROWS_TOK + place, -1)
        shuffle = jax.random.permutation(sub_key, ROWS_TOK)
        return values[jnp.argsort(shuffle)]
    dest = jax.vmap(one_source)(blocks, keys).reshape(ROWS).astype(jnp.int32)
    return (counts, dest)


def draw_counts(key, part):
    return packing(key)[0]


def draw_dest_index(key, part):
    return packing(key)[1]


def setup_inputs(seed: int = 0) -> dict:
    key_of = jax.random.split(jax.random.key(seed), 8)
    return {
        "teacher_rows": draw_teacher_rows(jax.random.fold_in(key_of[7], 71), 0),
        "drafter_rows": draw_drafter_rows(jax.random.fold_in(key_of[7], 71), 0),
        "head": draw_head(jax.random.fold_in(key_of[7], 71), 0),
        "fr_ids": draw_fr_ids(jax.random.fold_in(key_of[7], 71), 0),
        "targets": draw_targets(jax.random.fold_in(key_of[7], 71), 0),
        "dest_index": draw_dest_index(jax.random.fold_in(key_of[7], 71), 0),
        "counts": draw_counts(jax.random.fold_in(key_of[7], 71), 0),
    }


loss_scale = 16.0


def block_terms(operands, head, fr_ids):
    teach, draft, wanted, valid = operands
    teach_logit = jnp.dot(teach, head, preferred_element_type=jnp.float32)
    draft_logit = jnp.dot(draft, head, preferred_element_type=jnp.float32)
    teach_max = jnp.max(teach_logit, axis=1, keepdims=True)
    draft_max = jnp.max(draft_logit, axis=1, keepdims=True)
    teach_exp = jnp.exp(teach_logit - teach_max)
    draft_exp = jnp.exp(draft_logit - draft_max)
    teach_total = jnp.sum(teach_exp, axis=1)
    draft_total = jnp.sum(draft_exp, axis=1)
    cross = jnp.sum(teach_exp * (teach_logit - draft_logit), axis=1)
    hit_table = (wanted[:, None] == fr_ids[None, :]).astype(jnp.float32)
    hits = jnp.sum(hit_table, axis=1)
    target_logit = jnp.sum(hit_table * draft_logit, axis=1)
    teach_lse = teach_max[:, 0] + jnp.log(teach_total)
    draft_lse = draft_max[:, 0] + jnp.log(draft_total)
    row_loss = valid * (cross / teach_total - teach_lse + draft_lse + hits * (draft_lse - target_logit))
    teach_prob = teach_exp / teach_total[:, None]
    draft_prob = draft_exp / draft_total[:, None]
    grad_logit = (valid[:, None] * ((1.0 + hits)[:, None] * draft_prob - teach_prob - hit_table)).astype(jnp.bfloat16)
    summed = jnp.dot(grad_logit, head.T, preferred_element_type=jnp.float32)
    return row_loss, (loss_scale * summed).astype(jnp.bfloat16)


def reference(teacher_rows, drafter_rows, head, fr_ids, targets, dest_index, counts):
    spot = jnp.where(dest_index >= 0, dest_index, ROWS).astype(jnp.int32)
    moved = jnp.zeros((ROWS + 1, D), jnp.bfloat16).at[spot].set(teacher_rows)[:ROWS]
    places = jnp.arange(ROWS, dtype=jnp.int32)
    owner = (places // ROWS_TOK).astype(jnp.int32)
    valid = ((places % ROWS_TOK) < counts[owner]).astype(jnp.float32)
    block = 512 if ROWS % 512 == 0 else ROWS
    many = ROWS // block
    operands = (moved.reshape(many, block, D), drafter_rows.reshape(many, block, D),
                targets.reshape(many, block), valid.reshape(many, block))
    row_loss, drafter_grad = lax.map(lambda ops: block_terms(ops, head, fr_ids), operands)
    return row_loss.reshape(ROWS), drafter_grad.reshape(ROWS, D)
```

```python
import functools

import jax
import jax.numpy as jnp
from jax import lax
from jax.experimental import pallas as pl
from jax.experimental.pallas import tpu as pltpu
from jax.sharding import PartitionSpec as P

REACH = 4
CORES = 2
PAD = 8

loss_scale = 16.0

VM = pl.BlockSpec(memory_space=pltpu.VMEM)
SM = pl.BlockSpec(memory_space=pltpu.SMEM)


def call(body, outs, specs, name, flops=0, mib=8):
    return pl.pallas_call(
        body,
        out_shape=outs,
        in_specs=specs,
        out_specs=jax.tree.map(lambda _: VM, outs),
        name=name,
        cost_estimate=pl.CostEstimate(flops=flops, transcendentals=0, bytes_accessed=0),
        compiler_params=pltpu.CompilerParams(vmem_limit_bytes=mib << 20),
    )


def shape(dims, dtype=jnp.float32):
    return jax.ShapeDtypeStruct(dims, dtype)


def shifts_of(tok_size):
    return [0, 1, tok_size // 2, tok_size // 2 + 1]


def pack_body(tok_size, dest_ref, rows_ref, *outs):
    rows = rows_ref.shape[0]
    capacity = rows // REACH
    me = lax.axis_index("tok")
    dest = dest_ref[...]
    slot = lax.broadcasted_iota(jnp.int32, (capacity, rows), 0)
    for out, shift in zip(outs, shifts_of(tok_size)):
        low = lax.rem(me + shift, tok_size) * rows
        inside = (dest >= low) & (dest < low + rows)
        first = jnp.min(jnp.where(inside, dest - low, rows), axis=1, keepdims=True)
        place = jnp.where(inside, dest - low - first, -1)
        select = jnp.where(slot == place, 1.0, 0.0).astype(jnp.bfloat16)
        out[:capacity] = jnp.dot(select, rows_ref[...], preferred_element_type=jnp.float32).astype(jnp.bfloat16)
        out[capacity:] = jnp.broadcast_to(first.astype(jnp.float32), (PAD, out.shape[1])).astype(jnp.bfloat16)


def unpack_body(*refs):
    *parts, out = refs
    rows = out.shape[0]
    capacity = rows // REACH
    slot = lax.broadcasted_iota(jnp.int32, (rows, capacity), 0)
    rank = lax.broadcasted_iota(jnp.int32, (rows, capacity), 1)
    total = jnp.zeros(out.shape, jnp.float32)
    for part in parts:
        first = part[capacity:, :capacity].astype(jnp.float32).astype(jnp.int32)[:1]
        select = jnp.where(slot == rank + first, 1.0, 0.0).astype(jnp.bfloat16)
        total += jnp.dot(select, part[:capacity], preferred_element_type=jnp.float32)
    out[...] = total.astype(out.dtype)


def joined(mine, other, buf):
    width = mine.shape[1]
    core = lax.rem(lax.axis_index("voc"), CORES)
    buf[:, pl.ds(pl.multiple_of(core * width, width), width)] = mine[...]
    buf[:, pl.ds(pl.multiple_of((1 - core) * width, width), width)] = other[...]


def chip_rows(step, chips, depth):
    chip = lax.rem(lax.axis_index("voc") // CORES + chips - step, chips)
    return pl.ds(pl.multiple_of(chip * depth, depth), depth)


def blocks_of(width):
    size = min(1024, width)
    return [slice(i, i + size) for i in range(0, width, size)]


def first_body(step, chips, mine, other, head, out, buf):
    joined(mine, other, buf)
    rows = chip_rows(step, chips, buf.shape[1])
    for cols in blocks_of(out.shape[1]):
        out[:, cols] = jnp.dot(buf[...], head[rows, cols], preferred_element_type=jnp.float32)


def more_body(step, chips, mine, other, head, acc, out, buf):
    joined(mine, other, buf)
    rows = chip_rows(step, chips, buf.shape[1])
    for cols in blocks_of(out.shape[1]):
        out[:, cols] = acc[:, cols] + jnp.dot(buf[...], head[rows, cols], preferred_element_type=jnp.float32)


def lanes(block):
    return [block[:, i : i + 128] for i in range(0, block.shape[1], 128)]


def as_row(column):
    return jnp.broadcast_to(column, (column.shape[0], 8)).T[:1]


def as_column(row):
    return jnp.broadcast_to(row, (8, row.shape[1])).T[:, :1]


def draft_body(step, chips, mine, other, head, acc, ids, wanted, out, stats, buf):
    joined(mine, other, buf)
    depth = chip_rows(step, chips, buf.shape[1])
    count = out.shape[0]
    target = jnp.broadcast_to(as_column(wanted[...]), (count, 128))
    top = jnp.full((count, 128), -jnp.inf, jnp.float32)
    total = jnp.zeros((count, 128), jnp.float32)
    hits = jnp.zeros((count, 128), jnp.float32)
    picked = jnp.zeros((count, 128), jnp.float32)
    for cols in blocks_of(out.shape[1]):
        out[:, cols] = acc[:, cols] + jnp.dot(buf[...], head[depth, cols], preferred_element_type=jnp.float32)
        block = lanes(out[:, cols])
        above = functools.reduce(jnp.maximum, block, top)
        total = total * jnp.exp(top - above)
        top = above
        for piece, ident in zip(block, lanes(ids[:, cols])):
            total += jnp.exp(piece - top)
            same = target == ident
            hits += jnp.where(same, 1.0, 0.0)
            picked += jnp.where(same, piece, 0.0)
    peak = jnp.max(top, axis=1, keepdims=True)
    total = jnp.sum(total * jnp.exp(top - peak), axis=1, keepdims=True)
    stats[0:1] = as_row(peak)
    stats[1:2] = as_row(total)
    stats[2:3] = as_row(jnp.sum(picked, axis=1, keepdims=True))
    stats[3:4] = as_row(jnp.sum(hits, axis=1, keepdims=True))
    stats[4:] = jnp.zeros((4, count), jnp.float32)


def teach_body(step, chips, mine, other, head, acc, draft, known, out, stats, buf):
    joined(mine, other, buf)
    depth = chip_rows(step, chips, buf.shape[1])
    count = out.shape[0]
    top = jnp.full((count, 128), -jnp.inf, jnp.float32)
    total = jnp.zeros((count, 128), jnp.float32)
    cross = jnp.zeros((count, 128), jnp.float32)
    for cols in blocks_of(out.shape[1]):
        out[:, cols] = acc[:, cols] + jnp.dot(buf[...], head[depth, cols], preferred_element_type=jnp.float32)
        block = lanes(out[:, cols])
        above = functools.reduce(jnp.maximum, block, top)
        scale = jnp.exp(top - above)
        total = total * scale
        cross = cross * scale
        top = above
        for piece, drafted in zip(block, lanes(draft[:, cols])):
            weight = jnp.exp(piece - top)
            total += weight
            cross += weight * (piece - drafted)
    peak = jnp.max(top, axis=1, keepdims=True)
    scale = jnp.exp(top - peak)
    stats[0:4] = known[0:4]
    stats[4:5] = as_row(peak)
    stats[5:6] = as_row(jnp.sum(total * scale, axis=1, keepdims=True))
    stats[6:7] = as_row(jnp.sum(cross * scale, axis=1, keepdims=True))
    stats[7:] = jnp.zeros((1, count), jnp.float32)


def feature_rows(step, chips, other_core, width):
    me = lax.axis_index("voc")
    chip = lax.rem(me // CORES + step, chips)
    core = lax.rem(me, CORES)
    core = 1 - core if other_core else core
    return pl.ds(pl.multiple_of((chip * CORES + core) * width, width), width)


def grad_body(step, chips, parts, width, counts, *refs):
    every = [ref[...] for ref in refs[:parts]]
    draft, teach, ids, wanted, head, loss, grads, out = refs[parts:]
    count = draft.shape[0]
    here = [(s[0:1], s[1:2], s[2:3], s[3:4], s[4:5], s[5:6], s[6:7]) for s in every]
    draft_max = functools.reduce(jnp.maximum, [s[0] for s in here])
    teach_max = functools.reduce(jnp.maximum, [s[4] for s in here])
    draft_total = sum(s[1] * jnp.exp(s[0] - draft_max) for s in here)
    teach_total = sum(s[5] * jnp.exp(s[4] - teach_max) for s in here)
    cross = sum(s[6] * jnp.exp(s[4] - teach_max) for s in here)
    picked = sum(s[2] for s in here)
    hits = sum(s[3] for s in here)
    draft_lse = draft_max + jnp.log(draft_total)
    teach_lse = teach_max + jnp.log(teach_total)
    slots = lax.broadcasted_iota(jnp.int32, (1, count), 1)
    valid = slots < counts[0, lax.axis_index("tok")]
    row_loss = cross / teach_total - teach_lse + draft_lse + hits * (draft_lse - picked)
    loss[...] = jnp.where(valid, row_loss, 0.0)
    target = jnp.broadcast_to(as_column(wanted[...]), (count, 128))
    keep = jnp.where(valid, 1.0, 0.0)
    draft_shift = jnp.broadcast_to(as_column(draft_lse), (count, 128))
    teach_shift = jnp.broadcast_to(as_column(teach_lse), (count, 128))
    factor = jnp.broadcast_to(as_column(keep * (1.0 + hits)), (count, 128))
    keep = jnp.broadcast_to(as_column(keep), (count, 128))
    rows = feature_rows(step, chips, True, width)
    total = jnp.zeros(out.shape, jnp.float32)
    for cols in blocks_of(draft.shape[1]):
        for start in range(cols.start, cols.stop, 128):
            at = slice(start, start + 128)
            value = factor * jnp.exp(draft[:, at] - draft_shift) - keep * jnp.exp(teach[:, at] - teach_shift)
            value = value - jnp.where(target == ids[:, at], keep, 0.0)
            grads[:, at] = value.astype(jnp.bfloat16)
        total += lax.dot_general(
            grads[:, cols], head[rows, cols], (((1,), (1,)), ((), ())), preferred_element_type=jnp.float32
        )
    out[...] = total.astype(out.dtype)


def slice_body(step, chips, other_core, width, grads, head, out):
    rows = feature_rows(step, chips, other_core, width)
    out[...] = lax.dot_general(
        grads[...], head[rows, :], (((1,), (1,)), ((), ())), preferred_element_type=jnp.float32
    ).astype(out.dtype)


def per_device(teacher_rows, drafter_rows, head, fr_ids, targets, dest_index, counts):
    tok_size = lax.axis_size("tok")
    voc_size = lax.axis_size("voc")
    chips = voc_size // CORES
    rows, width = teacher_rows.shape
    features, columns = head.shape
    capacity = rows // REACH
    half = CORES * width
    flops = 2 * rows * columns * width

    def over_tok(block, distance):
        return lax.ppermute(block, "tok", [(i, (i + distance) % tok_size) for i in range(tok_size)])

    def over_chips(block, step):
        return lax.ppermute(block, "voc", [(i, (i + step * CORES) % voc_size) for i in range(voc_size)])

    def over_cores(block):
        return lax.ppermute(block, "voc", [(i, i + 1 - 2 * (i % CORES)) for i in range(voc_size)])

    head = pltpu.with_memory_space_constraint(head, pltpu.VMEM)
    ids = fr_ids.reshape(1, columns)
    wanted = targets.reshape(1, rows)

    parts = call(
        functools.partial(pack_body, tok_size),
        [shape((capacity + PAD, width), jnp.bfloat16)] * REACH,
        [VM, VM],
        "pack",
    )(dest_index.reshape(1, rows), teacher_rows)
    parts = [part if shift == 0 else over_tok(part, shift) for part, shift in zip(parts, shifts_of(tok_size))]
    moved = call(unpack_body, shape((rows, width), jnp.bfloat16), [VM] * REACH, "unpack")(*parts)

    def gathered(block):
        mine = [block] + [over_chips(block, step) for step in range(1, chips)]
        return [(piece, over_cores(piece)) for piece in mine]

    def partial(pairs, name):
        acc = None
        buf = [pltpu.VMEM((rows, half), jnp.bfloat16)]
        for step, (mine, other) in enumerate(pairs):
            body = first_body if acc is None else more_body
            acc = pl.pallas_call(
                functools.partial(body, step, chips),
                out_shape=shape((rows, columns)),
                in_specs=[VM] * (3 if acc is None else 4),
                out_specs=VM,
                scratch_shapes=buf,
                name=name + str(step),
                cost_estimate=pl.CostEstimate(flops=2 * flops, transcendentals=0, bytes_accessed=0),
                compiler_params=pltpu.CompilerParams(vmem_limit_bytes=12 << 20),
            )(mine, other, head, *([] if acc is None else [acc]))
        return acc

    def last(body, pair, acc, extra, name):
        return pl.pallas_call(
            functools.partial(body, chips - 1, chips),
            out_shape=[shape((rows, columns)), shape((8, rows))],
            in_specs=[VM] * (4 + len(extra)),
            out_specs=[VM, VM],
            scratch_shapes=[pltpu.VMEM((rows, half), jnp.bfloat16)],
            name=name,
            cost_estimate=pl.CostEstimate(flops=3 * flops, transcendentals=0, bytes_accessed=0),
            compiler_params=pltpu.CompilerParams(vmem_limit_bytes=12 << 20),
        )(*pair, head, acc, *extra)

    draft_pairs = gathered(drafter_rows)
    teach_pairs = gathered(moved)
    draft, known = last(draft_body, draft_pairs[-1], partial(draft_pairs[:-1], "draft"), (ids, wanted), "draft_last")
    teach, stats = last(teach_body, teach_pairs[-1], partial(teach_pairs[:-1], "teach"), (draft, known), "teach_last")

    every = [stats] + [over_chips(stats, step) for step in range(1, chips)]
    every = every + [over_cores(piece) for piece in every]

    step = 1 % chips
    loss, grads, sent = call(
        functools.partial(grad_body, step, chips, len(every), width),
        [shape((1, rows)), shape((rows, columns), jnp.bfloat16), shape((rows, width), jnp.bfloat16)],
        [SM] + [VM] * (len(every) + 5),
        "grad",
        2 * flops,
    )(counts.reshape(1, tok_size), *every, draft, teach, ids, wanted, head)

    def grad_slice(step, other_core, dtype):
        return call(
            functools.partial(slice_body, step, chips, other_core, width),
            shape((rows, width), dtype),
            [VM, VM],
            "slice%d_%d" % (step, other_core),
            flops,
        )(grads, head)

    arrived = []
    for step in range(1, chips):
        if step > 1:
            sent = grad_slice(step, True, jnp.bfloat16)
        own = grad_slice(step, False, jnp.float32)
        pair = (own + over_cores(sent).astype(jnp.float32)).astype(jnp.bfloat16)
        arrived.append(over_chips(pair, step))
    total = grad_slice(0, False, jnp.float32) + over_cores(grad_slice(0, True, jnp.bfloat16)).astype(jnp.float32)
    for piece in arrived:
        total = total + piece.astype(jnp.float32)
    return loss.reshape(rows), (loss_scale * total).astype(jnp.bfloat16)


def solution(mesh):
    return jax.shard_map(
        per_device,
        mesh=mesh,
        in_specs=(
            P("tok", "voc"),
            P("tok", "voc"),
            P(None, "voc"),
            P("voc"),
            P("tok"),
            P("tok"),
            P(),
        ),
        out_specs=(P("tok"), P("tok", "voc")),
        check_vma=False,
    )
```

```python
import functools

import jax
import jax.numpy as jnp
from jax import lax
from jax.experimental import pallas as pl
from jax.experimental.pallas import tpu as pltpu
from jax.sharding import PartitionSpec as P


REACH = 4
CORES = 2
PAD = 8
CHUNK = 32

loss_scale = 16.0

VM = pl.BlockSpec(memory_space=pltpu.VMEM)
HB = pl.BlockSpec(memory_space=pltpu.HBM)


def call(body, outs, specs, flops=0, mib=8):
    return pl.pallas_call(
        body,
        out_shape=outs,
        in_specs=specs,
        out_specs=jax.tree.map(lambda _: VM, outs),
        cost_estimate=pl.CostEstimate(flops=flops, transcendentals=0, bytes_accessed=0),
        compiler_params=pltpu.CompilerParams(vmem_limit_bytes=mib << 20),
    )


def shape(dims, dtype=jnp.float32):
    return jax.ShapeDtypeStruct(dims, dtype)


def shifts_of(tok_size):
    return [0, 1, tok_size // 2, tok_size // 2 + 1]


def pack_body(tok_size, dest_hbm, rows_hbm, draft_hbm, _, *refs):
    *outs, draft, dest_ref, rows_ref, sems = refs
    copies = [
        pltpu.make_async_copy(dest_hbm, dest_ref, sems.at[0]),
        pltpu.make_async_copy(rows_hbm, rows_ref, sems.at[1]),
        pltpu.make_async_copy(draft_hbm, draft, sems.at[2]),
    ]
    for copy in copies:
        copy.start()
    for copy in copies:
        copy.wait()
    rows = rows_ref.shape[0]
    capacity = rows // REACH
    me = lax.axis_index("tok")
    dest = dest_ref[...]
    slot = lax.broadcasted_iota(jnp.int32, (capacity, rows), 0)
    for out, shift in zip(outs, shifts_of(tok_size)):
        low = lax.rem(me + shift, tok_size) * rows
        inside = (dest >= low) & (dest < low + rows)
        first = jnp.min(jnp.where(inside, dest - low, rows), axis=1, keepdims=True) if shift else 0
        place = jnp.where(inside, dest - low - first, -1)
        select = jnp.where(slot == place, 1.0, 0.0).astype(jnp.bfloat16)
        out[:capacity] = jnp.dot(select, rows_ref[...], preferred_element_type=jnp.float32).astype(jnp.bfloat16)
        if shift:
            out[capacity:] = jnp.broadcast_to(first.astype(jnp.float32), (PAD, out.shape[1])).astype(jnp.bfloat16)


def unpack_body(nearest, *refs):
    *parts, out, rest = refs
    capacity = nearest.shape[0]
    rows = rest.shape[0]
    slot = capacity + lax.broadcasted_iota(jnp.int32, (rows, capacity), 0)
    rank = lax.broadcasted_iota(jnp.int32, (rows, capacity), 1)
    total = jnp.zeros(rest.shape, jnp.float32)
    for part in parts:
        first = part[capacity:, :capacity].astype(jnp.float32).astype(jnp.int32)[:1]
        select = jnp.where(slot == rank + first, 1.0, 0.0).astype(jnp.bfloat16)
        total += jnp.dot(select, part[:capacity], preferred_element_type=jnp.float32)
    out[:capacity] = nearest[...]
    rest[...] = total.astype(rest.dtype)
    out[capacity:] = total.astype(out.dtype)


def put(pieces, buf, cols=slice(None)):
    at = 0
    for piece in pieces:
        buf[at : at + piece.shape[0], cols] = piece[...]
        at += piece.shape[0]


def joined(refs, buf):
    pieces = len(refs) // CORES
    width = refs[0].shape[1]
    core = lax.rem(lax.axis_index("voc"), CORES)
    put(refs[:pieces], buf, pl.ds(pl.multiple_of(core * width, width), width))
    put(refs[pieces:], buf, pl.ds(pl.multiple_of((1 - core) * width, width), width))


def taken(accs, cols):
    width = accs[0].shape[1]
    at = cols.start // width
    return accs[at][:, cols.start - at * width : cols.stop - at * width]


def chip_rows(step, chips, depth):
    chip = lax.rem(lax.axis_index("voc") // CORES + chips - step, chips)
    return pl.ds(pl.multiple_of(chip * depth, depth), depth)


def blocks_of(width):
    size = min(1024, width)
    return [slice(i, i + size) for i in range(0, width, size)]


def partial_body(step, chips, pieces, base, *refs):
    head, *accs, out, buf = refs[CORES * pieces :]
    joined(refs[: CORES * pieces], buf)
    rows = chip_rows(step, chips, buf.shape[1])
    for cols in blocks_of(out.shape[1]):
        value = jnp.dot(
            buf[...], head[rows, base + cols.start : base + cols.stop], preferred_element_type=jnp.float32
        )
        out[:, cols] = taken(accs, cols) + value if accs else value


def single_body(step, chips, pieces, *refs):
    head, *accs, out, buf = refs[pieces:]
    put(refs[:pieces], buf)
    rows = feature_rows(chips - step, chips, False, buf.shape[1])
    for cols in blocks_of(out.shape[1]):
        out[:, cols] = taken(accs, cols) + jnp.dot(buf[...], head[rows, cols], preferred_element_type=jnp.float32)


def as_row(column):
    return jnp.broadcast_to(column, (column.shape[0], 8)).T[:1]


def as_column(row):
    return jnp.broadcast_to(row, (8, row.shape[1])).T[:, :1]


def spans(cols):
    return [slice(i, i + 128) for i in range(cols.start, cols.stop, 128)]


def chunks_of(count):
    return [slice(i, i + CHUNK) for i in range(0, count, CHUNK)]


def staggered(blocks, fill, use):
    for i in range(len(blocks) + 1):
        if i < len(blocks):
            fill(blocks[i])
        if i:
            use(blocks[i - 1])


def hits_body(ids, wanted, hits, target):
    count = target.shape[0]
    target[...] = jnp.broadcast_to(as_column(wanted[...]), target.shape)
    for some in chunks_of(count):
        found = jnp.zeros((CHUNK, 128), jnp.float32)
        for at in spans(slice(0, ids.shape[1])):
            found += jnp.where(target[some] == ids[:, at], 1.0, 0.0)
        hits[some] = found


def draft_body(step, chips, mine, other, head, hits, *refs):
    *acc, out, stats, buf, top, total = refs
    joined((mine, other), buf)
    rows = chip_rows(step, chips, buf.shape[1])
    count = out.shape[0]
    top[...] = jnp.full((count, 128), -jnp.inf, jnp.float32)
    total[...] = jnp.zeros((count, 128), jnp.float32)

    def fill(cols):
        value = jnp.dot(buf[...], head[rows, cols], preferred_element_type=jnp.float32)
        out[:, cols] = acc[0][:, cols] + value if acc else value

    def use(cols):
        for some in chunks_of(count):
            above = functools.reduce(jnp.maximum, [out[some, at] for at in spans(cols)], top[some])
            sums = total[some] * jnp.exp(top[some] - above)
            for at in spans(cols):
                sums += jnp.exp(out[some, at] - above)
            top[some], total[some] = above, sums

    staggered(blocks_of(out.shape[1]), fill, use)
    peak = jnp.max(top[...], axis=1, keepdims=True)
    stats[0:1] = as_row(peak)
    stats[1:2] = as_row(jnp.sum(total[...] * jnp.exp(top[...] - peak), axis=1, keepdims=True))
    stats[2:3] = as_row(jnp.sum(hits[...], axis=1, keepdims=True))
    stats[3:] = jnp.zeros((5, count), jnp.float32)


def teach_body(step, chips, pieces, *refs):
    head, known, acc, out, stats, buf, top, total = refs[pieces:]
    put(refs[:pieces], buf)
    rows = feature_rows(chips - step, chips, True, buf.shape[1])
    count = out.shape[0]
    top[...] = jnp.full((count, 128), -jnp.inf, jnp.float32)
    total[...] = jnp.zeros((count, 128), jnp.float32)

    def fill(cols):
        out[:, cols] = acc[:, cols] + jnp.dot(buf[...], head[rows, cols], preferred_element_type=jnp.float32)

    def use(cols):
        for some in chunks_of(count):
            above = functools.reduce(jnp.maximum, [out[some, at] for at in spans(cols)], top[some])
            sums = total[some] * jnp.exp(top[some] - above)
            for at in spans(cols):
                sums += jnp.exp(out[some, at] - above)
            top[some], total[some] = above, sums

    staggered(blocks_of(out.shape[1]), fill, use)
    peak = jnp.max(top[...], axis=1, keepdims=True)
    stats[0:3] = known[0:3]
    stats[3:4] = as_row(peak)
    stats[4:5] = as_row(jnp.sum(total[...] * jnp.exp(top[...] - peak), axis=1, keepdims=True))
    stats[5:] = jnp.zeros((3, count), jnp.float32)


def exps_body(draft, teach, stats, counts, drafted, taught, keep, kept):
    count = draft.shape[0]
    for source, out, row in ((draft, drafted, 0), (teach, taught, 3)):
        peak = jnp.broadcast_to(as_column(stats[row : row + 1]), (count, 128))
        for start in range(0, source.shape[1], 128):
            at = slice(start, start + 128)
            out[:, at] = jnp.exp(source[:, at] - peak)
    keep[...] = valid_rows(counts, count)
    kept[...] = jnp.broadcast_to(as_column(keep[...]), kept.shape)


def picked_body(draft, ids, target, picked):
    parts = []
    for some in chunks_of(draft.shape[0]):
        seen = jnp.zeros((CHUNK, 128), jnp.float32)
        for at in spans(slice(0, draft.shape[1])):
            seen += jnp.where(target[some] == ids[:, at], draft[some, at], 0.0)
        parts.append(jnp.sum(seen, axis=1, keepdims=True))
    picked[...] = as_row(jnp.concatenate(parts, axis=0))


def sums_body(draft, teach, taught, picked, stats, near, sums):
    count = draft.shape[0]
    parts = []
    for some in chunks_of(count):
        mixed = jnp.zeros((CHUNK, 128), jnp.float32)
        for at in spans(slice(0, draft.shape[1])):
            mixed += taught[some, at] * (teach[some, at] - draft[some, at])
        parts.append(jnp.sum(mixed, axis=1, keepdims=True))
    sums[0:1] = picked[...]
    peak = stats[3:4]
    sums[1:2] = as_row(jnp.concatenate(parts, axis=0)) * jnp.exp(peak - jnp.maximum(peak, near[3:4]))
    sums[2:] = jnp.zeros((6, count), jnp.float32)


def valid_rows(counts, count):
    spots = lax.broadcasted_iota(jnp.int32, counts.shape, 1)
    used = jnp.sum(jnp.where(spots == lax.axis_index("tok"), counts[...], 0), axis=1, keepdims=True)
    return jnp.where(lax.broadcasted_iota(jnp.int32, (1, count), 1) < used, 1.0, 0.0)


def merged(refs):
    here = [ref[...] for ref in refs]
    draft_max = functools.reduce(jnp.maximum, [s[0:1] for s in here])
    teach_max = functools.reduce(jnp.maximum, [s[3:4] for s in here])
    draft_total = sum(s[1:2] * jnp.exp(s[0:1] - draft_max) for s in here)
    teach_total = sum(s[4:5] * jnp.exp(s[3:4] - teach_max) for s in here)
    return draft_max, draft_total, teach_max, teach_total, sum(s[2:3] for s in here)


def close_body(chips, counts, own, other, *refs):
    *refs, loss, out = refs
    every, refs = refs[: CORES * chips], refs[CORES * chips :]
    pairs, arrived = refs[:chips], refs[chips:]
    total = own[...] + other[...].astype(jnp.float32)
    for piece in arrived:
        total += piece[...].astype(jnp.float32)
    out[...] = (loss_scale * total).astype(out.dtype)
    draft_max, draft_total, teach_max, teach_total, hits = merged(every)
    picked = sum(pair[0:1] for pair in pairs)
    cross = 0.0
    for chip, pair in enumerate(pairs):
        peak = functools.reduce(jnp.maximum, [ref[3:4] for ref in every[CORES * chip : CORES * (chip + 1)]])
        cross += pair[1:2] * jnp.exp(peak - teach_max)
    draft_lse = draft_max + jnp.log(draft_total)
    teach_lse = teach_max + jnp.log(teach_total)
    row_loss = cross / teach_total - teach_lse + draft_lse + hits * (draft_lse - picked)
    loss[...] = valid_rows(counts, loss.shape[1]) * row_loss


def feature_rows(step, chips, other_core, width):
    me = lax.axis_index("voc")
    chip = lax.rem(me // CORES + step, chips)
    core = lax.rem(me, CORES)
    core = 1 - core if other_core else core
    return pl.ds(pl.multiple_of((chip * CORES + core) * width, width), width)


def grad_body(step, chips, parts, width, *refs):
    every = refs[:parts]
    draft, teach, keep, kept, target, ids, head, grads, out = refs[parts:]
    count = draft.shape[0]
    draft_max, draft_total, teach_max, teach_total, hits = merged(every)
    draft_scale = keep[...] * (1.0 + hits) * (jnp.exp(every[0][0:1] - draft_max) / draft_total)
    teach_scale = keep[...] * (jnp.exp(every[0][3:4] - teach_max) / teach_total)
    draft_scale = jnp.broadcast_to(as_column(draft_scale), (count, 128))
    teach_scale = jnp.broadcast_to(as_column(teach_scale), (count, 128))
    rows = feature_rows(step, chips, True, width)
    total = jnp.zeros(out.shape, jnp.float32)
    for cols in blocks_of(draft.shape[1]):
        for row in range(0, count, CHUNK):
            some = slice(row, row + CHUNK)
            for start in range(cols.start, cols.stop, 128):
                at = slice(start, start + 128)
                value = draft_scale[some] * draft[some, at] - teach_scale[some] * teach[some, at]
                value = value - jnp.where(target[some] == ids[:, at], kept[some], 0.0)
                grads[some, at] = value.astype(jnp.bfloat16)
        total += lax.dot_general(
            grads[:, cols], head[rows, cols], (((1,), (1,)), ((), ())), preferred_element_type=jnp.float32
        )
    out[...] = total.astype(out.dtype)


def slice_body(step, chips, other_core, width, grads, head, out):
    rows = feature_rows(step, chips, other_core, width)
    out[...] = lax.dot_general(
        grads[...], head[rows, :], (((1,), (1,)), ((), ())), preferred_element_type=jnp.float32
    ).astype(out.dtype)


def per_device(teacher_rows, drafter_rows, head, fr_ids, targets, dest_index, counts):
    tok_size = lax.axis_size("tok")
    voc_size = lax.axis_size("voc")
    chips = voc_size // CORES
    rows, width = teacher_rows.shape
    _, columns = head.shape
    capacity = rows // REACH
    half = CORES * width
    flops = 2 * rows * columns * width

    def over_tok(block, distance):
        return lax.ppermute(block, "tok", [(i, (i + distance) % tok_size) for i in range(tok_size)])

    def over_chips(block, step):
        return lax.ppermute(block, "voc", [(i, (i + step * CORES) % voc_size) for i in range(voc_size)])

    def over_cores(block):
        return lax.ppermute(block, "voc", [(i, i + 1 - 2 * (i % CORES)) for i in range(voc_size)])

    def stay(array):
        return pltpu.with_memory_space_constraint(array, pltpu.HBM)

    ids = fr_ids.reshape(1, columns)
    wanted = targets.reshape(1, rows)

    pack = pl.pallas_call(
        functools.partial(pack_body, tok_size),
        out_shape=[
            shape((capacity + (PAD if shift else 0), width), jnp.bfloat16) for shift in shifts_of(tok_size)
        ]
        + [shape((rows, width), jnp.bfloat16)],
        in_specs=[HB] * 4,
        out_specs=[VM] * (REACH + 1),
        scratch_shapes=[
            pltpu.VMEM((1, rows), jnp.int32),
            pltpu.VMEM((rows, width), jnp.bfloat16),
            pltpu.SemaphoreType.DMA((3,)),
        ],
        name="pack",
        compiler_params=pltpu.CompilerParams(vmem_limit_bytes=8 << 20),
    )
    *parts, draft_mine = pack(stay(dest_index.reshape(1, rows)), stay(teacher_rows), stay(drafter_rows), stay(head))
    moves = {}
    for name in ("half", "next", "both"):
        at = {"half": 2, "next": 1, "both": 3}[name]
        moves[at] = over_tok(parts[at], shifts_of(tok_size)[at])
    parts = [parts[0]] + [moves[at] for at in range(1, REACH)]
    moved, rest = call(
        unpack_body, [shape((rows, width), jnp.bfloat16), shape((rows - capacity, width), jnp.bfloat16)], [VM] * REACH
    )(*parts)

    def gathered(block, start=0):
        pairs = []
        for step in range(start, chips):
            if step:
                piece = over_chips(block, step)
            else:
                piece = block
            pairs.append((piece, over_cores(piece)))
        return pairs

    whole = shape((rows, columns))
    buf = pltpu.VMEM((rows, half), jnp.bfloat16)
    lane = pltpu.VMEM((rows, 128), jnp.float32)
    step_flops = 2 * flops

    def kernel(body, outs, specs, scratch):
        return pl.pallas_call(
            body,
            out_shape=outs,
            in_specs=specs,
            out_specs=jax.tree.map(lambda _: VM, outs),
            scratch_shapes=scratch,
            cost_estimate=pl.CostEstimate(flops=step_flops, transcendentals=0, bytes_accessed=0),
            compiler_params=pltpu.CompilerParams(vmem_limit_bytes=12 << 20),
        )

    def partial(step, pairs, accs, base, size):
        args = [side for core in range(CORES) for side in (pair[core] for pair in pairs)]
        return kernel(
            functools.partial(partial_body, step, chips, len(pairs), base),
            shape((rows, size)),
            [VM] * (len(args) + 1 + len(accs)),
            [buf],
        )(*args, head, *accs)

    draft_pairs = gathered(drafter_rows)
    draft_pairs[0] = (draft_mine, draft_pairs[0][1])
    early_pairs = gathered(parts[0], 1)
    moved_other = over_cores(moved)
    teach_pairs = [(moved, moved_other)] + gathered(rest, 1)

    wide = shape((rows, 128))
    hits, target = kernel(hits_body, [wide, shape(wide.shape, jnp.int32)], [VM] * 2, [])(ids, wanted)
    accs = []
    for step, pair in enumerate(draft_pairs[:-1]):
        accs = [partial(step, [pair], accs, 0, columns)]
    draft, known = kernel(
        functools.partial(draft_body, chips - 1, chips),
        [whole, shape((8, rows))],
        [VM] * (4 + len(accs)),
        [buf] + [lane] * 2,
    )(*draft_pairs[-1], head, hits, *accs)

    half_columns = columns // 2
    accs = [partial(0, [teach_pairs[0]], [], i * half_columns, half_columns) for i in range(2)]
    for step in range(1, chips - 1):
        accs = [partial(step, [early_pairs[step - 1], teach_pairs[step]], accs, 0, columns)]
    mine, other = zip(early_pairs[-1], teach_pairs[-1])
    slim = pltpu.VMEM((rows, width), jnp.bfloat16)
    acc = kernel(
        functools.partial(single_body, chips - 1, chips, len(mine)), whole, [VM] * (len(mine) + 1 + len(accs)), [slim]
    )(*mine, head, *accs)
    teach, stats = kernel(
        functools.partial(teach_body, chips - 1, chips, len(other)),
        [whole, shape((8, rows))],
        [VM] * (len(other) + 3),
        [slim] + [lane] * 2,
    )(*other, head, known, acc)

    every = [piece for pair in gathered(stats) for piece in pair]
    used = counts.reshape(1, tok_size)
    drafted, taught, keep, kept = kernel(exps_body, [whole, whole, shape((1, rows)), wide], [VM] * 4, [])(
        draft, teach, stats, used
    )
    picked = kernel(picked_body, shape((1, rows)), [VM] * 3, [])(draft, ids, target)
    sums = kernel(sums_body, shape((8, rows)), [VM] * 6, [])(
        draft, teach, taught, picked, *every[:CORES]
    )

    grads, sent = kernel(
        functools.partial(grad_body, 1 % chips, chips, len(every), width),
        [shape((rows, columns), jnp.bfloat16), shape((rows, width), jnp.bfloat16)],
        [VM] * (len(every) + 7),
        [],
    )(*every, drafted, taught, keep, kept, target, ids, head)
    near = over_cores(sums)
    sums = sums + near
    pairs = [sums]
    for step in range(1, chips):
        pairs.append(over_chips(sums, step))

    def grad_slice(step, other_core, dtype):
        return kernel(
            functools.partial(slice_body, step, chips, other_core, width), shape((rows, width), dtype), [VM, VM], []
        )(grads, head)

    arrived = []
    for step in range(1, chips):
        if step > 1:
            sent = grad_slice(step, True, jnp.bfloat16)
        own = grad_slice(step, False, jnp.float32)
        other = over_cores(sent)
        pair = (own + other.astype(jnp.float32)).astype(jnp.bfloat16)
        arrived.append(over_chips(pair, step))
    other = over_cores(grad_slice(0, True, jnp.bfloat16))
    own = grad_slice(0, False, jnp.float32)
    loss, drafter_grad = kernel(
        functools.partial(close_body, chips),
        [shape((1, rows)), shape((rows, width), jnp.bfloat16)],
        [VM] * (3 + len(every) + len(pairs) + len(arrived)),
        [],
    )(used, own, other, *every, *pairs, *arrived)
    return loss.reshape(rows), drafter_grad


def solution(mesh):
    return jax.shard_map(
        per_device,
        mesh=mesh,
        in_specs=(
            P("tok", "voc"),
            P("tok", "voc"),
            P(None, "voc"),
            P("voc"),
            P("tok"),
            P("tok"),
            P(),
        ),
        out_specs=(P("tok"), P("tok", "voc")),
        check_vma=False,
    )
```

```python
import functools

import jax
import jax.numpy as jnp
from jax import lax
from jax.experimental import pallas as pl
from jax.experimental.pallas import tpu as pltpu
from jax.sharding import PartitionSpec as P


REACH = 4
CORES = 2
PAD = 8
CHUNK = 32

loss_scale = 16.0

VM = pl.BlockSpec(memory_space=pltpu.VMEM)
HB = pl.BlockSpec(memory_space=pltpu.HBM)


def call(body, outs, specs, flops=0, mib=8):
    return pl.pallas_call(
        body,
        out_shape=outs,
        in_specs=specs,
        out_specs=jax.tree.map(lambda _: VM, outs),
        cost_estimate=pl.CostEstimate(flops=flops, transcendentals=0, bytes_accessed=0),
        compiler_params=pltpu.CompilerParams(vmem_limit_bytes=mib << 20),
    )


def shape(dims, dtype=jnp.float32):
    return jax.ShapeDtypeStruct(dims, dtype)


def shifts_of(tok_size):
    return [0, 1, tok_size // 2, tok_size // 2 + 1]


def pack_body(tok_size, dest_hbm, rows_hbm, draft_hbm, _, *refs):
    *outs, draft, dest_ref, rows_ref, sems = refs
    copies = [
        pltpu.make_async_copy(dest_hbm, dest_ref, sems.at[0]),
        pltpu.make_async_copy(rows_hbm, rows_ref, sems.at[1]),
        pltpu.make_async_copy(draft_hbm, draft, sems.at[2]),
    ]
    for copy in copies:
        copy.start()
    for copy in copies:
        copy.wait()
    rows = rows_ref.shape[0]
    capacity = rows // REACH
    me = lax.axis_index("tok")
    dest = dest_ref[...]
    slot = lax.broadcasted_iota(jnp.int32, (capacity, rows), 0)
    for out, shift in zip(outs, shifts_of(tok_size)):
        low = lax.rem(me + shift, tok_size) * rows
        inside = (dest >= low) & (dest < low + rows)
        first = jnp.min(jnp.where(inside, dest - low, rows), axis=1, keepdims=True) if shift else 0
        place = jnp.where(inside, dest - low - first, -1)
        select = jnp.where(slot == place, 1.0, 0.0).astype(jnp.bfloat16)
        out[:capacity] = jnp.dot(select, rows_ref[...], preferred_element_type=jnp.float32).astype(jnp.bfloat16)
        if shift:
            out[capacity:] = jnp.broadcast_to(first.astype(jnp.float32), (PAD, out.shape[1])).astype(jnp.bfloat16)


def unpack_body(nearest, *refs):
    *parts, out, rest = refs
    capacity = nearest.shape[0]
    rows = rest.shape[0]
    slot = capacity + lax.broadcasted_iota(jnp.int32, (rows, capacity), 0)
    rank = lax.broadcasted_iota(jnp.int32, (rows, capacity), 1)
    total = jnp.zeros(rest.shape, jnp.float32)
    for part in parts:
        first = part[capacity:, :capacity].astype(jnp.float32).astype(jnp.int32)[:1]
        select = jnp.where(slot == rank + first, 1.0, 0.0).astype(jnp.bfloat16)
        total += jnp.dot(select, part[:capacity], preferred_element_type=jnp.float32)
    out[:capacity] = nearest[...]
    rest[...] = total.astype(rest.dtype)
    out[capacity:] = total.astype(out.dtype)


def put(pieces, buf, cols=slice(None)):
    at = 0
    for piece in pieces:
        buf[at : at + piece.shape[0], cols] = piece[...]
        at += piece.shape[0]


def joined(refs, buf):
    pieces = len(refs) // CORES
    width = refs[0].shape[1]
    core = lax.rem(lax.axis_index("voc"), CORES)
    put(refs[:pieces], buf, pl.ds(pl.multiple_of(core * width, width), width))
    put(refs[pieces:], buf, pl.ds(pl.multiple_of((1 - core) * width, width), width))


def taken(accs, cols):
    width = accs[0].shape[1]
    at = cols.start // width
    return accs[at][:, cols.start - at * width : cols.stop - at * width]


def chip_rows(step, chips, depth):
    chip = lax.rem(lax.axis_index("voc") // CORES + chips - step, chips)
    return pl.ds(pl.multiple_of(chip * depth, depth), depth)


def blocks_of(width, most=1024):
    size = min(most, width)
    return [slice(i, i + size) for i in range(0, width, size)]


def partial_body(step, chips, pieces, base, *refs):
    head, *accs, out, buf = refs[CORES * pieces :]
    joined(refs[: CORES * pieces], buf)
    rows = chip_rows(step, chips, buf.shape[1])
    for cols in blocks_of(out.shape[1]):
        value = jnp.dot(
            buf[...], head[rows, base + cols.start : base + cols.stop], preferred_element_type=jnp.float32
        )
        out[:, cols] = taken(accs, cols) + value if accs else value


def single_body(step, chips, pieces, *refs):
    head, top, total, hits, *accs, out, stats, buf = refs[pieces:]
    put(refs[:pieces], buf)
    rows = feature_rows(chips - step, chips, False, buf.shape[1])
    for cols in blocks_of(out.shape[1]):
        out[:, cols] = taken(accs, cols) + jnp.dot(buf[...], head[rows, cols], preferred_element_type=jnp.float32)
    peak = jnp.max(top[...], axis=1, keepdims=True)
    stats[0:1] = as_row(peak)
    stats[1:2] = as_row(jnp.sum(total[...] * jnp.exp(top[...] - peak), axis=1, keepdims=True))
    stats[2:3] = as_row(jnp.sum(hits[...], axis=1, keepdims=True))
    stats[3:] = jnp.zeros((5, out.shape[0]), jnp.float32)


def as_row(column):
    return jnp.broadcast_to(column, (column.shape[0], 8)).T[:1]


def as_column(row):
    return jnp.broadcast_to(row, (8, row.shape[1])).T[:, :1]


def spans(cols):
    return [slice(i, i + 128) for i in range(cols.start, cols.stop, 128)]


def chunks_of(count):
    return [slice(i, i + CHUNK) for i in range(0, count, CHUNK)]


def staggered(blocks, fill, use):
    for i in range(len(blocks) + 1):
        if i < len(blocks):
            fill(blocks[i])
        if i:
            use(blocks[i - 1])


def hits_body(ids, wanted, counts, struck, hits, keep):
    count = hits.shape[0]
    keep[...] = valid_rows(counts, count)
    target = jnp.broadcast_to(as_column(wanted[...]), (count, 128))
    kept = jnp.broadcast_to(as_column(keep[...]), (count, 128))
    for some in chunks_of(count):
        found = jnp.zeros((CHUNK, 128), jnp.float32)
        for at in spans(slice(0, ids.shape[1])):
            hit = jnp.where(target[some] == ids[:, at], kept[some], 0.0)
            struck[some, at] = hit
            found += hit
        hits[some] = found


def draft_body(step, chips, mine, other, head, *refs):
    *acc, out, top, total, buf = refs
    joined((mine, other), buf)
    rows = chip_rows(step, chips, buf.shape[1])
    count = out.shape[0]
    top[...] = jnp.full((count, 128), -jnp.inf, jnp.float32)
    total[...] = jnp.zeros((count, 128), jnp.float32)

    def fill(cols):
        value = jnp.dot(buf[...], head[rows, cols], preferred_element_type=jnp.float32)
        out[:, cols] = acc[0][:, cols] + value if acc else value

    def use(cols):
        for some in chunks_of(count):
            above = functools.reduce(jnp.maximum, [out[some, at] for at in spans(cols)], top[some])
            sums = total[some] * jnp.exp(top[some] - above)
            for at in spans(cols):
                sums += jnp.exp(out[some, at] - above)
            top[some], total[some] = above, sums

    staggered(blocks_of(out.shape[1]), fill, use)


def teach_body(step, chips, pieces, *refs):
    head, known, acc, out, stats, buf, top, total = refs[pieces:]
    put(refs[:pieces], buf)
    rows = feature_rows(chips - step, chips, True, buf.shape[1])
    count = out.shape[0]
    top[...] = jnp.full((count, 128), -jnp.inf, jnp.float32)
    total[...] = jnp.zeros((count, 128), jnp.float32)

    def fill(cols):
        out[:, cols] = acc[:, cols] + jnp.dot(buf[...], head[rows, cols], preferred_element_type=jnp.float32)

    def use(cols):
        for some in chunks_of(count):
            above = functools.reduce(jnp.maximum, [out[some, at] for at in spans(cols)], top[some])
            sums = total[some] * jnp.exp(top[some] - above)
            for at in spans(cols):
                sums += jnp.exp(out[some, at] - above)
            top[some], total[some] = above, sums

    staggered(blocks_of(out.shape[1], 2048), fill, use)
    peak = jnp.max(top[...], axis=1, keepdims=True)
    stats[0:3] = known[0:3]
    stats[3:4] = as_row(peak)
    stats[4:5] = as_row(jnp.sum(total[...] * jnp.exp(top[...] - peak), axis=1, keepdims=True))
    stats[5:] = jnp.zeros((3, count), jnp.float32)


def exps_body(draft, teach, stats, drafted, taught):
    count = draft.shape[0]
    for source, out, row in ((draft, drafted, 0), (teach, taught, 3)):
        peak = jnp.broadcast_to(as_column(stats[row : row + 1]), (count, 128))
        for start in range(0, source.shape[1], 128):
            at = slice(start, start + 128)
            out[:, at] = jnp.exp(source[:, at] - peak)


def picked_body(draft, struck, picked):
    parts = []
    for some in chunks_of(draft.shape[0]):
        seen = jnp.zeros((CHUNK, 128), jnp.float32)
        for at in spans(slice(0, draft.shape[1])):
            seen += struck[some, at] * draft[some, at]
        parts.append(jnp.sum(seen, axis=1, keepdims=True))
    picked[...] = as_row(jnp.concatenate(parts, axis=0))


def sums_body(draft, teach, taught, picked, stats, near, sums):
    count = draft.shape[0]
    parts = []
    for some in chunks_of(count):
        mixed = jnp.zeros((CHUNK, 128), jnp.float32)
        for at in spans(slice(0, draft.shape[1])):
            mixed += taught[some, at] * (teach[some, at] - draft[some, at])
        parts.append(jnp.sum(mixed, axis=1, keepdims=True))
    sums[0:1] = picked[...]
    peak = stats[3:4]
    sums[1:2] = as_row(jnp.concatenate(parts, axis=0)) * jnp.exp(peak - jnp.maximum(peak, near[3:4]))
    sums[2:] = jnp.zeros((6, count), jnp.float32)


def valid_rows(counts, count):
    spots = lax.broadcasted_iota(jnp.int32, counts.shape, 1)
    used = jnp.sum(jnp.where(spots == lax.axis_index("tok"), counts[...], 0), axis=1, keepdims=True)
    return jnp.where(lax.broadcasted_iota(jnp.int32, (1, count), 1) < used, 1.0, 0.0)


def merged(refs):
    here = [ref[...] for ref in refs]
    draft_max = functools.reduce(jnp.maximum, [s[0:1] for s in here])
    teach_max = functools.reduce(jnp.maximum, [s[3:4] for s in here])
    draft_total = sum(s[1:2] * jnp.exp(s[0:1] - draft_max) for s in here)
    teach_total = sum(s[4:5] * jnp.exp(s[3:4] - teach_max) for s in here)
    return draft_max, draft_total, teach_max, teach_total, sum(s[2:3] for s in here)


def terms_body(chips, counts, *refs):
    *every, terms = refs
    draft_max, draft_total, teach_max, teach_total, hits = merged(every)
    draft_lse = draft_max + jnp.log(draft_total)
    teach_lse = teach_max + jnp.log(teach_total)
    terms[0:1] = draft_lse - teach_lse + hits * draft_lse
    terms[1:2] = hits
    terms[2:3] = valid_rows(counts, terms.shape[1])
    for chip in range(chips):
        peak = functools.reduce(jnp.maximum, [ref[3:4] for ref in every[CORES * chip : CORES * (chip + 1)]])
        terms[3 + chip : 4 + chip] = jnp.exp(peak - teach_max) / teach_total


def close_body(chips, terms, own, other, *refs):
    *refs, loss, out = refs
    pairs, arrived = refs[:chips], refs[chips:]
    total = own[...] + other[...].astype(jnp.float32)
    for piece in arrived:
        total += piece[...].astype(jnp.float32)
    out[...] = (loss_scale * total).astype(out.dtype)
    row_loss = terms[0:1] - terms[1:2] * sum(pair[0:1] for pair in pairs)
    for chip, pair in enumerate(pairs):
        row_loss += pair[1:2] * terms[3 + chip : 4 + chip]
    loss[...] = terms[2:3] * row_loss


def feature_rows(step, chips, other_core, width):
    me = lax.axis_index("voc")
    chip = lax.rem(me // CORES + step, chips)
    core = lax.rem(me, CORES)
    core = 1 - core if other_core else core
    return pl.ds(pl.multiple_of((chip * CORES + core) * width, width), width)


def grad_body(step, chips, parts, width, *refs):
    every = refs[:parts]
    draft, teach, keep, struck, head, grads, out = refs[parts:]
    count = draft.shape[0]
    draft_max, draft_total, teach_max, teach_total, hits = merged(every)
    draft_scale = keep[...] * (1.0 + hits) * (jnp.exp(every[0][0:1] - draft_max) / draft_total)
    teach_scale = keep[...] * (jnp.exp(every[0][3:4] - teach_max) / teach_total)
    draft_scale = jnp.broadcast_to(as_column(draft_scale), (count, 128))
    teach_scale = jnp.broadcast_to(as_column(teach_scale), (count, 128))
    rows = feature_rows(step, chips, True, width)
    total = jnp.zeros(out.shape, jnp.float32)
    for cols in blocks_of(draft.shape[1]):
        for row in range(0, count, CHUNK):
            some = slice(row, row + CHUNK)
            for start in range(cols.start, cols.stop, 128):
                at = slice(start, start + 128)
                value = draft_scale[some] * draft[some, at] - teach_scale[some] * teach[some, at]
                grads[some, at] = (value - struck[some, at]).astype(jnp.bfloat16)
        total += lax.dot_general(
            grads[:, cols], head[rows, cols], (((1,), (1,)), ((), ())), preferred_element_type=jnp.float32
        )
    out[...] = total.astype(out.dtype)


def slice_body(step, chips, other_core, width, grads, head, out):
    rows = feature_rows(step, chips, other_core, width)
    out[...] = lax.dot_general(
        grads[...], head[rows, :], (((1,), (1,)), ((), ())), preferred_element_type=jnp.float32
    ).astype(out.dtype)


def per_device(teacher_rows, drafter_rows, head, fr_ids, targets, dest_index, counts):
    tok_size = lax.axis_size("tok")
    voc_size = lax.axis_size("voc")
    chips = voc_size // CORES
    rows, width = teacher_rows.shape
    _, columns = head.shape
    capacity = rows // REACH
    half = CORES * width
    flops = 2 * rows * columns * width

    def over_tok(block, distance):
        return lax.ppermute(block, "tok", [(i, (i + distance) % tok_size) for i in range(tok_size)])

    def over_chips(block, step):
        return lax.ppermute(block, "voc", [(i, (i + step * CORES) % voc_size) for i in range(voc_size)])

    def over_cores(block):
        return lax.ppermute(block, "voc", [(i, i + 1 - 2 * (i % CORES)) for i in range(voc_size)])

    def stay(array):
        return pltpu.with_memory_space_constraint(array, pltpu.HBM)

    ids = fr_ids.reshape(1, columns)
    wanted = targets.reshape(1, rows)

    pack = pl.pallas_call(
        functools.partial(pack_body, tok_size),
        out_shape=[
            shape((capacity + (PAD if shift else 0), width), jnp.bfloat16) for shift in shifts_of(tok_size)
        ]
        + [shape((rows, width), jnp.bfloat16)],
        in_specs=[HB] * 4,
        out_specs=[VM] * (REACH + 1),
        scratch_shapes=[
            pltpu.VMEM((1, rows), jnp.int32),
            pltpu.VMEM((rows, width), jnp.bfloat16),
            pltpu.SemaphoreType.DMA((3,)),
        ],
        name="pack",
        compiler_params=pltpu.CompilerParams(vmem_limit_bytes=8 << 20),
    )
    *parts, draft_mine = pack(stay(dest_index.reshape(1, rows)), stay(teacher_rows), stay(drafter_rows), stay(head))
    moves = {}
    for name in ("half", "next", "both"):
        at = {"half": 2, "next": 1, "both": 3}[name]
        moves[at] = over_tok(parts[at], shifts_of(tok_size)[at])
    parts = [parts[0]] + [moves[at] for at in range(1, REACH)]
    moved, rest = call(
        unpack_body, [shape((rows, width), jnp.bfloat16), shape((rows - capacity, width), jnp.bfloat16)], [VM] * REACH
    )(*parts)

    def gathered(block, start=0):
        pairs = []
        for step in range(start, chips):
            if step:
                piece = over_chips(block, step)
            else:
                piece = block
            pairs.append((piece, over_cores(piece)))
        return pairs

    whole = shape((rows, columns))
    buf = pltpu.VMEM((rows, half), jnp.bfloat16)
    lane = pltpu.VMEM((rows, 128), jnp.float32)
    step_flops = 2 * flops

    def kernel(body, outs, specs, scratch):
        return pl.pallas_call(
            body,
            out_shape=outs,
            in_specs=specs,
            out_specs=jax.tree.map(lambda _: VM, outs),
            scratch_shapes=scratch,
            cost_estimate=pl.CostEstimate(flops=step_flops, transcendentals=0, bytes_accessed=0),
            compiler_params=pltpu.CompilerParams(vmem_limit_bytes=12 << 20),
        )

    def partial(step, pairs, accs, base, size):
        args = [side for core in range(CORES) for side in (pair[core] for pair in pairs)]
        return kernel(
            functools.partial(partial_body, step, chips, len(pairs), base),
            shape((rows, size)),
            [VM] * (len(args) + 1 + len(accs)),
            [buf],
        )(*args, head, *accs)

    draft_pairs = gathered(drafter_rows)
    draft_pairs[0] = (draft_mine, draft_pairs[0][1])
    early_pairs = gathered(parts[0], 1)
    moved_other = over_cores(moved)
    teach_pairs = [(moved, moved_other)] + gathered(rest, 1)

    wide = shape((rows, 128))
    used = counts.reshape(1, tok_size)
    struck, hits, keep = kernel(hits_body, [whole, wide, shape((1, rows))], [VM] * 3, [])(ids, wanted, used)
    accs = []
    for step, pair in enumerate(draft_pairs[:-1]):
        accs = [partial(step, [pair], accs, 0, columns)]
    draft, top, total = kernel(
        functools.partial(draft_body, chips - 1, chips), [whole, wide, wide], [VM] * (3 + len(accs)), [buf]
    )(*draft_pairs[-1], head, *accs)

    half_columns = columns // 2
    accs = [partial(0, [teach_pairs[0]], [], i * half_columns, half_columns) for i in range(2)]
    for step in range(1, chips - 1):
        accs = [partial(step, [early_pairs[step - 1], teach_pairs[step]], accs, 0, columns)]
    mine, other = zip(early_pairs[-1], teach_pairs[-1])
    slim = pltpu.VMEM((rows, width), jnp.bfloat16)
    acc, known = kernel(
        functools.partial(single_body, chips - 1, chips, len(mine)),
        [whole, shape((8, rows))],
        [VM] * (len(mine) + 4 + len(accs)),
        [slim],
    )(*mine, head, top, total, hits, *accs)
    teach, stats = kernel(
        functools.partial(teach_body, chips - 1, chips, len(other)),
        [whole, shape((8, rows))],
        [VM] * (len(other) + 3),
        [slim] + [lane] * 2,
    )(*other, head, known, acc)

    every = [piece for pair in gathered(stats) for piece in pair]
    drafted, taught = kernel(exps_body, [whole, whole], [VM] * 3, [])(draft, teach, stats)
    picked = kernel(picked_body, shape((1, rows)), [VM] * 2, [])(draft, struck)
    sums = kernel(sums_body, shape((8, rows)), [VM] * 6, [])(
        draft, teach, taught, picked, *every[:CORES]
    )

    grads, sent = kernel(
        functools.partial(grad_body, 1 % chips, chips, len(every), width),
        [shape((rows, columns), jnp.bfloat16), shape((rows, width), jnp.bfloat16)],
        [VM] * (len(every) + 5),
        [],
    )(*every, drafted, taught, keep, struck, head)
    near = over_cores(sums)
    sums = sums + near
    pairs = [sums]
    for step in range(1, chips):
        pairs.append(over_chips(sums, step))

    def grad_slice(step, other_core, dtype):
        return kernel(
            functools.partial(slice_body, step, chips, other_core, width), shape((rows, width), dtype), [VM, VM], []
        )(grads, head)

    arrived = []
    for step in range(1, chips):
        if step > 1:
            sent = grad_slice(step, True, jnp.bfloat16)
        own = grad_slice(step, False, jnp.float32)
        other = over_cores(sent)
        pair = (own + other.astype(jnp.float32)).astype(jnp.bfloat16)
        arrived.append(over_chips(pair, step))
    other = over_cores(grad_slice(0, True, jnp.bfloat16))
    own = grad_slice(0, False, jnp.float32)
    terms = kernel(
        functools.partial(terms_body, chips), shape((3 + chips, rows)), [VM] * (1 + len(every)), []
    )(used, *every)
    loss, drafter_grad = kernel(
        functools.partial(close_body, chips),
        [shape((1, rows)), shape((rows, width), jnp.bfloat16)],
        [VM] * (3 + len(pairs) + len(arrived)),
        [],
    )(terms, own, other, *pairs, *arrived)
    return loss.reshape(rows), drafter_grad


def solution(mesh):
    return jax.shard_map(
        per_device,
        mesh=mesh,
        in_specs=(
            P("tok", "voc"),
            P("tok", "voc"),
            P(None, "voc"),
            P("voc"),
            P("tok"),
            P("tok"),
            P(),
        ),
        out_specs=(P("tok"), P("tok", "voc")),
        check_vma=False,
    )
```
